512 devices in a mesh: req: 64 (over x, z), tp: 8 (over y, core).
Axes of the slice: x: 4, y: 4, z: 16, core: 2. Of those that a mesh axis runs over, the one named last changes fastest.
Arguments:
- hidden: bfloat16 [8192, 1280], P(('req', 'tp')), may hold values from -6 to 6
- gate_weight: bfloat16 [1280, 4096], P(None, 'tp'), may hold values from -0.15625 to 0.15625
- up_weight: bfloat16 [1280, 4096], P(None, 'tp'), may hold values from -0.15625 to 0.15625
- down_weight: bfloat16 [4096, 1280], P('tp'), may hold values from -0.09375 to 0.09375
- gate_scale: float32 [4096], P('tp'), may hold values from 0.1 to 1.9
- up_scale: float32 [4096], P('tp'), may hold values from 0.1 to 1.9
- update_step_size: float32 [1280], replicated, may hold values from 0.05 to 0.6
- adapter_down_maps: bfloat16 [64, 1280, 16], P('req'), may hold values from -0.15625 to 0.15625
- adapter_up_maps: bfloat16 [64, 16, 4096], P('req', None, 'tp'), may hold values from -1.5 to 1.5
- lengths: int32 [512], P('req'), may hold values from 9 to 16, as said below
- request_adapter_index: int32 [512], P('req'), may hold values from 0 to 63, as said below
Outputs:
- updated: bfloat16 [8192, 1280], P(('req', 'tp'))
The draws below stay inside these ranges and needn't reach their ends.
Inputs may be any that keep to these rules, and one draw needn't show every extreme that they name: `request_adapter_index`: among the 8 requests of one index of req no adapter id occurs more than 1 times; one adapter occurs exactly 1 times on every index of req. `lengths`: on every index of req some request has length 16: those served by the adapter that every index uses.
All inputs are finite; a program needn't handle non-finite values.
Results may differ from the reference program's by a relative error of at most 0.003.
Values may be sent and summed in bfloat16 or wider, within the bound.
A program may use at most 64 MiB of HBM per device.

```python
import math
import jax
import jax.numpy as jnp
from jax import lax

MODEL_WIDTH = 1280
HIDDEN_WIDTH = 4096
ADAPTER_RANK = 16
SEQ_DEV = 8
PAD_LEN = 16
ADAPTER_TOTAL = 64
REQUESTS = 512
TOKENS = 8192
N_REQ = 64


def route_pair(key):
    base_key = jax.random.fold_in(key, 4111)
    keys = jax.random.split(base_key, 5)
    per_owner = max(1, SEQ_DEV // N_REQ)
    hot_adapter = jax.random.randint(keys[0], (), 0, ADAPTER_TOTAL)
    perm_keys = jax.random.split(keys[2], N_REQ)
    others = jax.vmap(lambda sub_key: jax.random.permutation(sub_key, ADAPTER_TOTAL - 1))(perm_keys)
    others = others.astype(jnp.int32)
    others = others + (others >= hot_adapter).astype(jnp.int32)
    repeated = jnp.tile(others, (1, per_owner))[:, :SEQ_DEV - per_owner]
    hot_cols = jnp.zeros((N_REQ, per_owner), jnp.int32) + hot_adapter
    combined = jnp.concatenate([hot_cols, repeated], axis=1)
    shuffle_keys = jax.random.split(keys[1], N_REQ)
    identity = jax.vmap(lambda sub_key, row: jax.random.permutation(sub_key, row))(shuffle_keys, combined)
    is_hot = identity == hot_adapter
    first_draw = jax.random.randint(keys[3], (N_REQ, SEQ_DEV), 0, PAD_LEN)
    second_draw = jax.random.randint(keys[4], (N_REQ, SEQ_DEV), 0, PAD_LEN)
    length_table = PAD_LEN - first_draw * second_draw // (2 * PAD_LEN)
    length_table = jnp.where(is_hot, PAD_LEN, length_table)
    return (length_table.reshape(REQUESTS).astype(jnp.int32), identity.reshape(REQUESTS).astype(jnp.int32))


def draw_lengths(key, part):
    return route_pair(key)[0]


def draw_request_adapter_index(key, part):
    return route_pair(key)[1]


def shard_levels(rng, dims, pieces, smallest, high):
    factor_of, own = 1.0, jax.random.fold_in(rng, 6)
    for position, shards_of in pieces:
        heights = jnp.exp(jax.random.uniform(jax.random.fold_in(own, position), (shards_of,), jnp.float32, smallest / len(pieces), high / len(pieces)))
        factor_of = factor_of * jnp.repeat(heights, dims[position] // shards_of).reshape([-1 if axis == position else 1 for axis in range(len(dims))])
    return factor_of


def bell_draw(stream_key, extent, deviation, most, cuts=(), dtype=jnp.bfloat16):
    loudness = shard_levels(stream_key, extent, cuts, -0.22, 0.18) if cuts else 1.0
    values = jax.random.normal(stream_key, extent, jnp.float32) * deviation * loudness
    return jnp.minimum(jnp.maximum(values, -most), most).astype(dtype)


def setup_inputs(seed: int = 0) -> dict:
    seeds = jax.random.split(jax.random.key(seed), 12)
    hidden = bell_draw(seeds[0], (TOKENS, MODEL_WIDTH), 1.0, 6.0, ((0, 512),))
    gate_weight = bell_draw(seeds[1], (MODEL_WIDTH, HIDDEN_WIDTH), MODEL_WIDTH ** -0.5, 0.15625, ((1, 8),))
    up_weight = bell_draw(seeds[2], (MODEL_WIDTH, HIDDEN_WIDTH), MODEL_WIDTH ** -0.5, 0.15625, ((1, 8),))
    down_weight = bell_draw(seeds[3], (HIDDEN_WIDTH, MODEL_WIDTH), HIDDEN_WIDTH ** -0.5, 0.09375, ((0, 8),))
    gate_scale = jnp.clip(1.0 + 0.18 * jax.random.normal(seeds[4], (HIDDEN_WIDTH,), jnp.float32), 0.1, 1.9)
    up_scale = jnp.clip(1.0 + 0.18 * jax.random.normal(seeds[5], (HIDDEN_WIDTH,), jnp.float32), 0.1, 1.9)
    update_step_size = jnp.clip(jnp.exp(jax.random.uniform(seeds[6], (MODEL_WIDTH,), jnp.float32, math.log(0.05), math.log(0.6))), 0.05, 0.6)
    adapter_down_maps = bell_draw(seeds[7], (ADAPTER_TOTAL, MODEL_WIDTH, ADAPTER_RANK), MODEL_WIDTH ** -0.5, 0.15625, ((0, 64),))
    adapter_up_maps = bell_draw(seeds[8], (ADAPTER_TOTAL, ADAPTER_RANK, HIDDEN_WIDTH), ADAPTER_RANK ** -0.5, 1.5, ((0, 64), (2, 8)))
    lengths = draw_lengths(jax.random.fold_in(seeds[11], 71), 0)
    request_adapter_index = draw_request_adapter_index(jax.random.fold_in(seeds[11], 71), 0)
    return dict(hidden=hidden, gate_weight=gate_weight, up_weight=up_weight, down_weight=down_weight, gate_scale=gate_scale, up_scale=up_scale, update_step_size=update_step_size, adapter_down_maps=adapter_down_maps, adapter_up_maps=adapter_up_maps, lengths=lengths, request_adapter_index=request_adapter_index)


def rms_norm(values):
    return values * lax.rsqrt(lax.optimization_barrier(jnp.mean(values * values, axis=-1, keepdims=True)) + 1e-06)

def reference(hidden, gate_weight, up_weight, down_weight, gate_scale, up_scale, update_step_size, adapter_down_maps, adapter_up_maps, lengths, request_adapter_index):
    blocks = hidden.reshape(N_REQ, SEQ_DEV * PAD_LEN, MODEL_WIDTH)
    block_lengths = lengths.reshape(N_REQ, SEQ_DEV)
    block_ids = request_adapter_index.reshape(N_REQ, SEQ_DEV)

    def one_block(operands):
        rows, lens, adapter_index = operands
        live_mask = (jnp.arange(PAD_LEN)[None, :] < lens[:, None]).astype(jnp.float32)
        gate_pre = jnp.dot(rows, gate_weight, preferred_element_type=jnp.float32) * gate_scale
        masked = rows.astype(jnp.float32).reshape(SEQ_DEV, PAD_LEN, MODEL_WIDTH) * live_mask[:, :, None]
        chosen_down_maps = adapter_down_maps[adapter_index].astype(jnp.float32)
        chosen_up_maps = adapter_up_maps[adapter_index].astype(jnp.float32)
        shrink = jnp.einsum('sjd,sdr->sjr', masked, chosen_down_maps, precision=lax.Precision.HIGHEST).astype(jnp.bfloat16)
        delta = jnp.einsum('sjr,srf->sjf', shrink.astype(jnp.float32), chosen_up_maps, precision=lax.Precision.HIGHEST).astype(jnp.bfloat16)
        delta = delta.reshape(SEQ_DEV * PAD_LEN, HIDDEN_WIDTH).astype(jnp.float32)
        up_pre = (jnp.dot(rows, up_weight, preferred_element_type=jnp.float32) + 0.5 * delta) * up_scale
        inner = (jax.nn.silu(gate_pre) * up_pre).astype(jnp.bfloat16)
        branch = jnp.dot(inner, down_weight, preferred_element_type=jnp.float32)
        start_state = rms_norm(rows.astype(jnp.float32))
        mixed = start_state + update_step_size * (rms_norm(branch) - start_state)
        live_rows = live_mask.reshape(SEQ_DEV * PAD_LEN)
        return (rms_norm(mixed) * live_rows[:, None]).astype(jnp.bfloat16)
    result = lax.map(one_block, (blocks, block_lengths, block_ids))
    return result.reshape(TOKENS, MODEL_WIDTH)
```

```python
import jax
import jax.numpy as jnp
from jax import lax
from jax.sharding import PartitionSpec as P


def rms_norm(values):
    return values * lax.rsqrt(jnp.mean(values * values, axis=-1, keepdims=True) + 1e-06)


def body(
    hidden,
    gate_weight,
    up_weight,
    down_weight,
    gate_scale,
    up_scale,
    update_step_size,
    adapter_down_maps,
    adapter_up_maps,
    lengths,
    request_adapter_index,
):
    owners = lax.axis_size("req")
    tp_count = lax.axis_size("tp")
    tp_index = lax.axis_index("tp")
    rank, columns = adapter_up_maps.shape[1:]
    features = hidden.shape[1]
    slice_width = features // tp_count
    down_slice = lax.dynamic_slice_in_dim(
        adapter_down_maps[0].T, tp_index * slice_width, slice_width, 1
    )
    up_all = lax.all_gather(adapter_up_maps[0], "req", axis=0, tiled=True)
    down_all = lax.all_gather(down_slice, "req", axis=0, tiled=True)
    gathered = lax.all_gather(hidden, "tp", axis=0, tiled=True)
    seq_count = lengths.shape[0]
    token_count = gathered.shape[0]
    pad_length = token_count // seq_count
    live_mask = jnp.arange(pad_length)[None, :] < lengths[:, None]
    token_ids = jnp.repeat(request_adapter_index, pad_length)
    chosen = token_ids[:, None] == jnp.arange(owners)[None, :]
    chosen = chosen & live_mask.reshape(token_count)[:, None]
    chosen = jnp.repeat(chosen, rank, axis=1)
    token_slice = lax.dynamic_slice_in_dim(gathered, tp_index * slice_width, slice_width, 1)
    partial = lax.dot_general(
        token_slice, down_all, (((1,), (1,)), ((), ())), preferred_element_type=jnp.float32
    )
    partial = jnp.sum(jnp.where(chosen, partial, 0.0).reshape(token_count, owners, rank), axis=1)
    shrink = lax.psum(partial, "tp").astype(jnp.bfloat16)
    spread = jnp.where(chosen, jnp.tile(shrink, (1, owners)), jnp.bfloat16(0))
    delta_rows = (
        jnp.dot(spread, up_all, preferred_element_type=jnp.float32)
        .astype(jnp.bfloat16)
        .astype(jnp.float32)
    )
    gate_pre = jnp.dot(gathered, gate_weight, preferred_element_type=jnp.float32) * gate_scale
    up_pre = (
        jnp.dot(gathered, up_weight, preferred_element_type=jnp.float32) + 0.5 * delta_rows
    ) * up_scale
    hidden_units = (jax.nn.silu(gate_pre) * up_pre).astype(jnp.bfloat16)
    row_share = token_count // tp_count
    row_start = tp_index * row_share
    branch = lax.psum_scatter(
        jnp.dot(hidden_units, down_weight, preferred_element_type=jnp.float32),
        "tp",
        scatter_dimension=0,
        tiled=True,
    )
    start_state = rms_norm(hidden.astype(jnp.float32))
    blended = start_state + update_step_size * (rms_norm(branch) - start_state)
    live_rows = lax.dynamic_slice_in_dim(
        live_mask.reshape(token_count).astype(jnp.float32), row_start, row_share, 0
    )
    return (rms_norm(blended) * live_rows[:, None]).astype(jnp.bfloat16)


def solution(mesh):
    placed = (
        P(("req", "tp"), None),
        P(None, "tp"),
        P(None, "tp"),
        P("tp", None),
        P("tp"),
        P("tp"),
        P(),
        P("req", None, None),
        P("req", None, "tp"),
        P("req"),
        P("req"),
    )
    return jax.shard_map(
        body, mesh=mesh, in_specs=placed, out_specs=P(("req", "tp"), None), check_vma=False
    )
```

```python
import functools

import jax
import jax.numpy as jnp
from jax import lax
from jax.experimental import pallas as pl
from jax.experimental.pallas import tpu as pltpu
from jax.sharding import PartitionSpec as P

MESH = pl.DeviceIdType.MESH
NX, NZ = 4, 16
EPS = 1e-06


def rms_norm(values):
    return values * lax.rsqrt(jnp.mean(values * values, axis=-1, keepdims=True) + EPS)


def kernel(
    tp_count,
    hidden_ref,
    gate_hbm,
    up_hbm,
    down_hbm,
    gate_scale_ref,
    up_scale_ref,
    step_ref,
    down_map_ref,
    up_map_ref,
    lengths_ref,
    ids_ref,
    out_ref,
    tokens,
    gate_w,
    up_w,
    down_w,
    gate_pre,
    up_base,
    maps,
    sums_out,
    sums_in,
    part_out,
    part_in,
    load_sem,
    tok_send,
    tok_recv,
    map_send,
    map_recv,
    sum_send,
    sum_recv,
    part_send,
    part_recv,
):
    me_r = lax.axis_index("req")
    me_t = lax.axis_index("tp")
    x = me_r // NZ
    z = lax.rem(me_r, NZ)
    pad, features = hidden_ref.shape
    rank, columns = up_map_ref.shape
    owners = maps.shape[0]
    window = maps.shape[2] - columns
    token_count = tp_count * pad
    peers = [lax.rem(me_t + k, tp_count) for k in range(1, tp_count)]

    def at(dx, dz):
        return lax.rem(x + dx + NX, NX) * NZ + lax.rem(z + dz + NZ, NZ)

    barrier = pltpu.get_barrier_semaphore()
    for peer in peers:
        pl.semaphore_signal(barrier, inc=1, device_id=(me_r, peer), device_id_type=MESH)
    for dx, dz in ((0, 1), (0, -1), (1, 0), (-1, 0)):
        pl.semaphore_signal(barrier, inc=1, device_id=(at(dx, dz), me_t), device_id_type=MESH)

    loads = [
        pltpu.make_async_copy(source, target, load_sem.at[i])
        for i, (source, target) in enumerate(
            ((gate_hbm, gate_w), (up_hbm, up_w), (down_hbm, down_w))
        )
    ]
    for load in loads:
        load.start()

    share = features // tp_count
    start = pl.multiple_of((me_t * share) // 128 * 128, 128)
    offset = me_t * share - start
    down_part = down_map_ref[pl.ds(start, window), :].astype(jnp.float32).T
    lane = lax.broadcasted_iota(jnp.int32, (rank, window), 1)
    down_part = jnp.where((lane >= offset) & (lane < offset + share), down_part, 0.0)
    maps[me_r, :, :columns] = up_map_ref[...]
    maps[me_r, :, columns:] = down_part.astype(jnp.bfloat16)
    own_rows = pl.ds(pl.multiple_of(me_t * pad, pad), pad)
    tokens[own_rows, :] = hidden_ref[...]

    lane = lax.broadcasted_iota(jnp.int32, (1, token_count), 1)
    token_ids = jnp.full((1, token_count), -1, jnp.int32)
    for s in range(tp_count):
        inside = (lane >= s * pad) & (lane < s * pad + lengths_ref[s])
        token_ids = jnp.where(inside, ids_ref[s], token_ids)
    owner_ids = lax.broadcasted_iota(jnp.int32, (owners, 1, token_count), 0)
    chosen = owner_ids == token_ids[None]

    pl.semaphore_wait(barrier, tp_count - 1 + 4)

    def to_peers(source, target, send_sem, recv_sem):
        copies = []
        for k, peer in enumerate(peers):
            copies.append(
                pltpu.make_async_remote_copy(
                    src_ref=source(peer),
                    dst_ref=target(me_t),
                    send_sem=send_sem.at[k],
                    recv_sem=recv_sem.at[me_t],
                    device_id=(me_r, peer),
                    device_id_type=MESH,
                )
            )
            copies[-1].start()
        return copies

    def from_peers(source, target, send_sem, recv_sem):
        for k, peer in enumerate(peers):
            pltpu.make_async_remote_copy(
                src_ref=source(peer),
                dst_ref=target(peer),
                send_sem=send_sem.at[k],
                recv_sem=recv_sem.at[peer],
                device_id=(me_r, peer),
                device_id_type=MESH,
            ).wait_recv()

    map_copies = []

    def map_copy(slot, device, index):
        return pltpu.make_async_remote_copy(
            src_ref=maps.at[slot],
            dst_ref=maps.at[slot],
            send_sem=map_send.at[index],
            recv_sem=map_recv.at[slot],
            device_id=(device, me_t),
            device_id_type=MESH,
        )

    def send_map(slot, device):
        copy = map_copy(slot, device, len(map_copies))
        map_copies.append(copy)
        copy.start()

    def wait_map(slot):
        map_copy(slot, at(0, 1), 0).wait_recv()

    token_args = (
        lambda peer: hidden_ref,
        lambda t: tokens.at[pl.ds(pl.multiple_of(t * pad, pad), pad)],
        tok_send,
        tok_recv,
    )
    half = NZ // 2
    z_next, z_last, x_next, x_last = at(0, 1), at(0, -1), at(1, 0), at(-1, 0)

    def z_step(s):
        minus, plus = s <= half, 0 < s < half
        if s > 0:
            wait_map(at(0, -s))
        if s < half:
            send_map(at(0, -s), z_next)
        if plus:
            wait_map(at(0, s))
        if s < half - 1:
            send_map(at(0, s), z_last)
        for dz in ((-s, s) if plus else (-s,)):
            send_map(at(0, dz), x_next)
            send_map(at(0, dz), x_last)

    def x_step(s):
        plus = 0 < s < half
        for dz in ((-s, s) if plus else (-s,)):
            wait_map(at(-1, dz))
            if dz <= 0:
                send_map(at(-1, dz), x_next)
            wait_map(at(1, dz))
            if dz > 0:
                send_map(at(1, dz), x_last)

    z_step(0)
    token_copies = to_peers(*token_args)
    for s in range(1, half + 1):
        z_step(s)
        x_step(s - 1)
        if s == 1:
            from_peers(*token_args)
            loads[0].wait()
            gate_pre[...] = jnp.dot(tokens[...], gate_w[...], preferred_element_type=jnp.float32)
        if s == 2:
            loads[1].wait()
            up_base[...] = jnp.dot(tokens[...], up_w[...], preferred_element_type=jnp.float32)
        if s == 3:
            v = gate_pre[...] * gate_scale_ref[...]
            gate_pre[...] = v / (1.0 + jnp.exp(-v))
    x_step(half)
    for s in range(half + 1):
        for dz in ((-s, s) if 0 < s < half else (-s,)):
            wait_map(at(2, dz))

    token_share = tokens[:, pl.ds(start, window)]
    products = lax.dot_general(
        maps[:, :, columns:].reshape(owners * rank, window),
        token_share,
        (((1,), (1,)), ((), ())),
        preferred_element_type=jnp.float32,
    ).reshape(owners, rank, token_count)
    partial = jnp.sum(jnp.where(chosen, products, 0.0), axis=0)
    sums_out[...] = partial
    sum_args = (lambda peer: sums_out, lambda t: sums_in.at[t], sum_send, sum_recv)
    sum_copies = to_peers(*sum_args)
    from_peers(*sum_args)
    shrink = partial
    for peer in peers:
        shrink = shrink + sums_in[peer]
    shrink = shrink.astype(jnp.bfloat16).astype(jnp.float32)
    spread = jnp.where(chosen, shrink[None], 0.0).astype(jnp.bfloat16)
    delta = lax.dot_general(
        spread.reshape(owners * rank, token_count),
        maps[:, :, :columns].reshape(owners * rank, columns),
        (((0,), (0,)), ((), ())),
        preferred_element_type=jnp.float32,
    )
    delta = delta.astype(jnp.bfloat16).astype(jnp.float32)
    up_pre = (up_base[...] + 0.5 * delta) * up_scale_ref[...]
    inner = (gate_pre[...] * up_pre).astype(jnp.bfloat16)
    loads[2].wait()
    gate_rows = jnp.dot(inner, down_w[...], preferred_element_type=jnp.float32)
    part_out[...] = gate_rows.astype(jnp.bfloat16).reshape(tp_count, pad, features)
    part_args = (lambda peer: part_out.at[peer], lambda t: part_in.at[t], part_send, part_recv)
    part_copies = to_peers(*part_args)

    begin = rms_norm(hidden_ref[...].astype(jnp.float32))
    branch = part_out[me_t].astype(jnp.float32)
    from_peers(*part_args)
    for peer in peers:
        branch = branch + part_in[peer].astype(jnp.float32)
    mixed = begin + step_ref[...] * (rms_norm(branch) - begin)
    row = lax.broadcasted_iota(jnp.int32, (pad, features), 0)
    out_ref[...] = jnp.where(row < lengths_ref[me_t], rms_norm(mixed), 0.0).astype(jnp.bfloat16)
    for copy in token_copies + sum_copies + part_copies + map_copies:
        copy.wait_send()


def body(
    hidden,
    gate_weight,
    up_weight,
    down_weight,
    gate_scale,
    up_scale,
    update_step_size,
    adapter_down_maps,
    adapter_up_maps,
    lengths,
    request_adapter_index,
):
    tp_count = lax.axis_size("tp")
    owners = lax.axis_size("req")
    pad, features = hidden.shape
    rank, columns = adapter_up_maps.shape[1:]
    token_count = tp_count * pad
    bf16, f32 = jnp.bfloat16, jnp.float32
    vmem = pl.BlockSpec(memory_space=pltpu.VMEM)
    smem = pl.BlockSpec(memory_space=pltpu.SMEM)
    hbm = pl.BlockSpec(memory_space=pl.ANY)
    dma = pltpu.SemaphoreType.DMA
    return pl.pallas_call(
        functools.partial(kernel, tp_count),
        out_shape=jax.ShapeDtypeStruct((pad, features), bf16),
        in_specs=[vmem, hbm, hbm, hbm, vmem, vmem, vmem, vmem, vmem, smem, smem],
        out_specs=vmem,
        scratch_shapes=[
            pltpu.VMEM((token_count, features), bf16),
            pltpu.VMEM(gate_weight.shape, bf16),
            pltpu.VMEM(up_weight.shape, bf16),
            pltpu.VMEM(down_weight.shape, bf16),
            pltpu.VMEM((token_count, columns), f32),
            pltpu.VMEM((token_count, columns), f32),
            pltpu.VMEM((owners, rank, columns + 256), bf16),
            pltpu.VMEM((rank, token_count), f32),
            pltpu.VMEM((tp_count, rank, token_count), f32),
            pltpu.VMEM((tp_count, pad, features), bf16),
            pltpu.VMEM((tp_count, pad, features), bf16),
            dma((3,)),
            dma((tp_count - 1,)),
            dma((tp_count,)),
            dma((owners - 1,)),
            dma((owners,)),
            dma((tp_count - 1,)),
            dma((tp_count,)),
            dma((tp_count - 1,)),
            dma((tp_count,)),
        ],
        compiler_params=pltpu.CompilerParams(
            collective_id=0, has_side_effects=True, vmem_limit_bytes=40 * 1024 * 1024
        ),
    )(
        hidden,
        gate_weight,
        up_weight,
        down_weight,
        gate_scale[None],
        up_scale[None],
        update_step_size[None],
        adapter_down_maps[0],
        adapter_up_maps[0],
        lengths,
        request_adapter_index,
    )


def solution(mesh):
    placed = (
        P(("req", "tp"), None),
        P(None, "tp"),
        P(None, "tp"),
        P("tp", None),
        P("tp"),
        P("tp"),
        P(),
        P("req", None, None),
        P("req", None, "tp"),
        P("req"),
        P("req"),
    )
    return jax.shard_map(
        body, mesh=mesh, in_specs=placed, out_specs=P(("req", "tp"), None), check_vma=False
    )
```

```python
import functools

import jax
import jax.numpy as jnp
from jax import lax
from jax.experimental import pallas as pl
from jax.experimental.pallas import tpu as pltpu
from jax.sharding import PartitionSpec as P

MESH = pl.DeviceIdType.MESH
NX, NZ = 4, 16
STRIDE = 4
EPS = 1e-06


def rms_norm(values):
    return values * lax.rsqrt(jnp.mean(values * values, axis=-1, keepdims=True) + EPS)


def kernel(
    tp_count,
    hidden_hbm,
    gate_hbm,
    up_hbm,
    down_hbm,
    gate_scale_hbm,
    up_scale_hbm,
    step_hbm,
    down_map_hbm,
    up_map_hbm,
    lengths_hbm,
    ids_hbm,
    out_ref,
    tokens,
    gate_w,
    up_w,
    down_w,
    gate_scale_ref,
    up_scale_ref,
    step_ref,
    lengths_ref,
    ids_ref,
    gate_pre,
    up_base,
    downs,
    ups,
    sums_out,
    sums_in,
    part_out,
    part_in,
    load_sem,
    tok_send,
    tok_recv,
    down_send,
    down_recv,
    up_send,
    up_recv,
    sum_send,
    sum_recv,
    part_send,
    part_recv,
):
    me_r = lax.axis_index("req")
    me_t = lax.axis_index("tp")
    x = me_r // NZ
    z = lax.rem(me_r, NZ)
    pad, features = hidden_hbm.shape
    rank, columns = up_map_hbm.shape
    owners, _, window = downs.shape
    token_count = tp_count * pad
    peers = [lax.rem(me_t + k, tp_count) for k in range(1, tp_count)]

    def at(dx, dz):
        return lax.rem(x + dx + NX, NX) * NZ + lax.rem(z + dz + NZ, NZ)

    barrier = pltpu.get_barrier_semaphore()
    for peer in peers:
        pl.semaphore_signal(barrier, inc=1, device_id=(me_r, peer), device_id_type=MESH)
    near = [(0, sign * d) for d in range(1, STRIDE + 1) for sign in (1, -1)] + [(1, 0), (-1, 0)]
    for dx, dz in near:
        pl.semaphore_signal(barrier, inc=1, device_id=(at(dx, dz), me_t), device_id_type=MESH)

    share = features // tp_count
    start = pl.multiple_of((me_t * share) // 128 * 128, 128)
    offset = me_t * share - start
    own_rows = pl.ds(pl.multiple_of(me_t * pad, pad), pad)
    loads = [
        pltpu.make_async_copy(source, target, load_sem.at[i])
        for i, (source, target) in enumerate(
            (
                (gate_hbm, gate_w),
                (up_hbm, up_w),
                (down_hbm, down_w),
                (hidden_hbm, tokens.at[own_rows]),
                (up_map_hbm, ups.at[me_r]),
                (down_map_hbm.at[:, pl.ds(start, window)], downs.at[me_r]),
                (lengths_hbm, lengths_ref),
                (ids_hbm, ids_ref),
                (gate_scale_hbm, gate_scale_ref),
                (up_scale_hbm, up_scale_ref),
                (step_hbm, step_ref),
            )
        )
    ]
    for i in (3, 4, 5, 6, 7, 8, 9, 10, 0, 1, 2):
        loads[i].start()
    for i in (6, 7, 8, 9, 10):
        loads[i].wait()

    lane = lax.broadcasted_iota(jnp.int32, (1, token_count), 1)
    token_ids = jnp.full((1, token_count), -1, jnp.int32)
    for s in range(tp_count):
        inside = (lane >= s * pad) & (lane < s * pad + lengths_ref[s])
        token_ids = jnp.where(inside, ids_ref[s], token_ids)
    owner_ids = lax.broadcasted_iota(jnp.int32, (owners, 1, token_count), 0)
    chosen = owner_ids == token_ids[None]

    for i in (3, 4, 5):
        loads[i].wait()
    pl.semaphore_wait(barrier, tp_count - 1 + len(near))

    def to_peers(source, target, send_sem, recv_sem):
        copies = []
        for k, peer in enumerate(peers):
            copies.append(
                pltpu.make_async_remote_copy(
                    src_ref=source(peer),
                    dst_ref=target(me_t),
                    send_sem=send_sem.at[k],
                    recv_sem=recv_sem.at[me_t],
                    device_id=(me_r, peer),
                    device_id_type=MESH,
                )
            )
            copies[-1].start()
        return copies

    def from_peers(source, target, send_sem, recv_sem):
        for k, peer in enumerate(peers):
            pltpu.make_async_remote_copy(
                src_ref=source(peer),
                dst_ref=target(peer),
                send_sem=send_sem.at[k],
                recv_sem=recv_sem.at[peer],
                device_id=(me_r, peer),
                device_id_type=MESH,
            ).wait_recv()

    kinds = ((downs, down_send, down_recv, []), (ups, up_send, up_recv, []))
    down, up = kinds

    def map_copy(kind, slot, device, index):
        blocks, send_sem, recv_sem, _ = kind
        return pltpu.make_async_remote_copy(
            src_ref=blocks.at[slot],
            dst_ref=blocks.at[slot],
            send_sem=send_sem.at[index],
            recv_sem=recv_sem.at[slot],
            device_id=(device, me_t),
            device_id_type=MESH,
        )

    def send_map(kind, slot, device):
        copy = map_copy(kind, slot, device, len(kind[3]))
        kind[3].append(copy)
        copy.start()

    def wait_map(kind, slot):
        map_copy(kind, slot, at(0, 1), 0).wait_recv()

    token_args = (
        lambda peer: tokens.at[own_rows],
        lambda t: tokens.at[pl.ds(pl.multiple_of(t * pad, pad), pad)],
        tok_send,
        tok_recv,
    )
    half = NZ // 2
    x_next, x_last = at(1, 0), at(-1, 0)
    stages = -(-half // STRIDE)
    arrived = set()

    def wait_once(kind, dz):
        if dz != 0 and (id(kind), dz) not in arrived:
            arrived.add((id(kind), dz))
            wait_map(kind, at(0, dz))

    def z_send(kind, stage):
        base = stage * STRIDE
        for sign, reach in ((1, half), (-1, half - 1)):
            steps = range(min(base + STRIDE, reach), base, -1)
            if len(steps):
                wait_once(kind, -sign * base)
            for to in steps:
                send_map(kind, at(0, -sign * base), at(0, sign * (to - base)))

    def members(stage):
        if stage == 0:
            return [0]
        near = range((stage - 1) * STRIDE + 1, min(stage * STRIDE, half) + 1)
        return [dz for d in near for dz in ((-d, d) if d < half else (-d,))]

    def x_send(kind, stage):
        for dz in members(stage):
            wait_once(kind, dz)
            send_map(kind, at(0, dz), x_next)
            send_map(kind, at(0, dz), x_last)

    def x_pass(kind, stage):
        for dz in members(stage):
            wait_map(kind, at(-1, dz))
            if dz <= 0:
                send_map(kind, at(-1, dz), x_next)
            wait_map(kind, at(1, dz))
            if dz > 0:
                send_map(kind, at(1, dz), x_last)

    def x_finish(kind):
        for stage in range(stages + 1):
            for dz in members(stage):
                wait_map(kind, at(2, dz))

    for kind in kinds:
        z_send(kind, 0)
    token_copies = to_peers(*token_args)
    for kind in kinds:
        x_send(kind, 0)
    for stage in range(1, stages + 1):
        for kind in kinds:
            z_send(kind, stage)
        for kind in kinds:
            x_send(kind, stage)
        if stage == stages:
            break
        for kind in kinds:
            x_pass(kind, stage - 1)
        if stage == stages - 1:
            from_peers(*token_args)
            loads[0].wait()
            v = jnp.dot(tokens[...], gate_w[...], preferred_element_type=jnp.float32)
            v = v * gate_scale_ref[...][None]
            gate_pre[...] = v / (1.0 + jnp.exp(-v))
            loads[1].wait()
            up_base[...] = jnp.dot(tokens[...], up_w[...], preferred_element_type=jnp.float32)
    for stage in (stages - 1, stages):
        x_pass(down, stage)
    x_pass(up, stages - 1)
    x_finish(down)

    lane = lax.broadcasted_iota(jnp.int32, (token_count, window), 1)
    token_share = tokens[:, pl.ds(start, window)].astype(jnp.float32)
    token_share = jnp.where((lane >= offset) & (lane < offset + share), token_share, 0.0)
    token_share = token_share.astype(jnp.bfloat16)
    products = lax.dot_general(
        downs[...].reshape(owners * rank, window),
        token_share,
        (((1,), (1,)), ((), ())),
        preferred_element_type=jnp.float32,
    ).reshape(owners, rank, token_count)
    partial = jnp.sum(jnp.where(chosen, products, 0.0), axis=0)
    sums_out[...] = partial
    sum_args = (lambda peer: sums_out, lambda t: sums_in.at[t], sum_send, sum_recv)
    sum_copies = to_peers(*sum_args)
    x_pass(up, stages)
    x_finish(up)
    from_peers(*sum_args)
    shrink = partial
    for peer in peers:
        shrink = shrink + sums_in[peer]
    shrink = shrink.astype(jnp.bfloat16).astype(jnp.float32)
    spread = jnp.where(chosen, shrink[None], 0.0).astype(jnp.bfloat16)
    delta = lax.dot_general(
        spread.reshape(owners * rank, token_count),
        ups[...].reshape(owners * rank, columns),
        (((0,), (0,)), ((), ())),
        preferred_element_type=jnp.float32,
    )
    delta = delta.astype(jnp.bfloat16).astype(jnp.float32)
    up_pre = (up_base[...] + 0.5 * delta) * up_scale_ref[...][None]
    inner = (gate_pre[...] * up_pre).astype(jnp.bfloat16)
    loads[2].wait()
    gate_rows = jnp.dot(inner, down_w[...], preferred_element_type=jnp.float32)
    part_out[...] = gate_rows.astype(jnp.bfloat16).reshape(tp_count, pad, features)
    part_args = (lambda peer: part_out.at[peer], lambda t: part_in.at[t], part_send, part_recv)
    part_copies = to_peers(*part_args)

    begin = rms_norm(tokens[own_rows, :].astype(jnp.float32))
    branch = part_out[me_t].astype(jnp.float32)
    from_peers(*part_args)
    for peer in peers:
        branch = branch + part_in[peer].astype(jnp.float32)
    mixed = begin + step_ref[...][None] * (rms_norm(branch) - begin)
    row = lax.broadcasted_iota(jnp.int32, (pad, features), 0)
    out_ref[...] = jnp.where(row < lengths_ref[me_t], rms_norm(mixed), 0.0).astype(jnp.bfloat16)
    for copy in token_copies + sum_copies + part_copies + down[3] + up[3]:
        copy.wait_send()


def body(
    hidden,
    gate_weight,
    up_weight,
    down_weight,
    gate_scale,
    up_scale,
    update_step_size,
    adapter_down_maps,
    adapter_up_maps,
    lengths,
    request_adapter_index,
):
    tp_count = lax.axis_size("tp")
    owners = lax.axis_size("req")
    pad, features = hidden.shape
    rank, columns = adapter_up_maps.shape[1:]
    token_count = tp_count * pad
    bf16, f32 = jnp.bfloat16, jnp.float32
    vmem = pl.BlockSpec(memory_space=pltpu.VMEM)
    hbm = pl.BlockSpec(memory_space=pl.ANY)
    dma = pltpu.SemaphoreType.DMA
    return pl.pallas_call(
        functools.partial(kernel, tp_count),
        out_shape=jax.ShapeDtypeStruct((pad, features), bf16),
        in_specs=[hbm] * 11,
        out_specs=vmem,
        scratch_shapes=[
            pltpu.VMEM((token_count, features), bf16),
            pltpu.VMEM(gate_weight.shape, bf16),
            pltpu.VMEM(up_weight.shape, bf16),
            pltpu.VMEM(down_weight.shape, bf16),
            pltpu.VMEM(gate_scale.shape, f32),
            pltpu.VMEM(up_scale.shape, f32),
            pltpu.VMEM(update_step_size.shape, f32),
            pltpu.SMEM(lengths.shape, jnp.int32),
            pltpu.SMEM(lengths.shape, jnp.int32),
            pltpu.VMEM((token_count, columns), f32),
            pltpu.VMEM((token_count, columns), f32),
            pltpu.VMEM((owners, rank, 256), bf16),
            pltpu.VMEM((owners, rank, columns), bf16),
            pltpu.VMEM((rank, token_count), f32),
            pltpu.VMEM((tp_count, rank, token_count), f32),
            pltpu.VMEM((tp_count, pad, features), bf16),
            pltpu.VMEM((tp_count, pad, features), bf16),
            dma((11,)),
            dma((tp_count - 1,)),
            dma((tp_count,)),
            dma((owners - 1,)),
            dma((owners,)),
            dma((owners - 1,)),
            dma((owners,)),
            dma((tp_count - 1,)),
            dma((tp_count,)),
            dma((tp_count - 1,)),
            dma((tp_count,)),
        ],
        compiler_params=pltpu.CompilerParams(
            collective_id=0, has_side_effects=True, vmem_limit_bytes=67000000
        ),
    )(
        hidden,
        gate_weight,
        up_weight,
        down_weight,
        gate_scale,
        up_scale,
        update_step_size,
        adapter_down_maps.transpose(0, 2, 1)[0],
        adapter_up_maps[0],
        lengths,
        request_adapter_index,
    )


def solution(mesh):
    placed = (
        P(("req", "tp"), None),
        P(None, "tp"),
        P(None, "tp"),
        P("tp", None),
        P("tp"),
        P("tp"),
        P(),
        P("req", None, None),
        P("req", None, "tp"),
        P("req"),
        P("req"),
    )
    return jax.shard_map(
        body, mesh=mesh, in_specs=placed, out_specs=P(("req", "tp"), None), check_vma=False
    )
```

```python
import functools

import jax
import jax.numpy as jnp
from jax import lax
from jax.experimental import pallas as pl
from jax.experimental.pallas import tpu as pltpu
from jax.sharding import PartitionSpec as P

MESH = pl.DeviceIdType.MESH
NX, NZ = 4, 16
STRIDE = 2
EPS = 1e-06


def rms_norm(values):
    return values * lax.rsqrt(jnp.mean(values * values, axis=-1, keepdims=True) + EPS)


def kernel(
    tp_count,
    hidden_hbm,
    gate_hbm,
    up_hbm,
    down_hbm,
    gate_scale_hbm,
    up_scale_hbm,
    step_hbm,
    down_map_hbm,
    up_map_hbm,
    lengths_hbm,
    ids_hbm,
    out_ref,
    tokens,
    gate_w,
    up_w,
    down_w,
    gate_scale_ref,
    up_scale_ref,
    step_ref,
    lengths_ref,
    ids_ref,
    gate_pre,
    up_base,
    downs,
    ups,
    sums_out,
    sums_in,
    part_out,
    part_in,
    load_sem,
    tok_send,
    tok_recv,
    down_send,
    down_recv,
    up_send,
    up_recv,
    sum_send,
    sum_recv,
    part_send,
    part_recv,
):
    me_r = lax.axis_index("req")
    me_t = lax.axis_index("tp")
    x = me_r // NZ
    z = lax.rem(me_r, NZ)
    pad, features = hidden_hbm.shape
    rank, columns = up_map_hbm.shape
    owners, _, window = downs.shape
    token_count = tp_count * pad
    y, core = me_t // 2, lax.rem(me_t, 2)
    hops = [(dy, other) for dy in (2, 1, 3) for other in (0, 1)] + [(0, 1)]
    peers = [lax.rem(y + dy, tp_count // 2) * 2 + lax.rem(core + other, 2) for dy, other in hops]

    def at(dx, dz):
        return lax.rem(x + dx + NX, NX) * NZ + lax.rem(z + dz + NZ, NZ)

    barrier = pltpu.get_barrier_semaphore()
    for peer in peers:
        pl.semaphore_signal(barrier, inc=1, device_id=(me_r, peer), device_id_type=MESH)
    near = [(0, sign * d) for d in range(1, STRIDE + 1) for sign in (1, -1)] + [(1, 0), (-1, 0), (2, 0)]
    for dx, dz in near:
        pl.semaphore_signal(barrier, inc=1, device_id=(at(dx, dz), me_t), device_id_type=MESH)

    share = features // tp_count
    start = pl.multiple_of((me_t * share) // 128 * 128, 128)
    offset = me_t * share - start
    own_rows = pl.ds(pl.multiple_of(me_t * pad, pad), pad)
    loads = [
        pltpu.make_async_copy(source, target, load_sem.at[i])
        for i, (source, target) in enumerate(
            (
                (gate_hbm, gate_w),
                (up_hbm, up_w),
                (down_hbm, down_w),
                (hidden_hbm, tokens.at[own_rows]),
                (up_map_hbm, ups.at[me_r]),
                (down_map_hbm.at[:, pl.ds(start, window)], downs.at[me_r]),
                (lengths_hbm, lengths_ref),
                (ids_hbm, ids_ref),
                (gate_scale_hbm, gate_scale_ref),
                (up_scale_hbm, up_scale_ref),
                (step_hbm, step_ref),
            )
        )
    ]
    for i in (3, 4, 5, 6, 7, 8, 9, 10, 0, 1, 2):
        loads[i].start()
    for i in (6, 7, 8, 9, 10):
        loads[i].wait()

    lane = lax.broadcasted_iota(jnp.int32, (1, token_count), 1)
    token_ids = jnp.full((1, token_count), -1, jnp.int32)
    for s in range(tp_count):
        inside = (lane >= s * pad) & (lane < s * pad + lengths_ref[s])
        token_ids = jnp.where(inside, ids_ref[s], token_ids)
    owner_ids = lax.broadcasted_iota(jnp.int32, (owners, 1, token_count), 0)
    chosen = owner_ids == token_ids[None]

    for i in (3, 4, 5):
        loads[i].wait()
    pl.semaphore_wait(barrier, tp_count - 1 + len(near))

    def to_peers(source, target, send_sem, recv_sem):
        copies = []
        for k, peer in enumerate(peers):
            copies.append(
                pltpu.make_async_remote_copy(
                    src_ref=source(peer),
                    dst_ref=target(me_t),
                    send_sem=send_sem.at[k],
                    recv_sem=recv_sem.at[me_t],
                    device_id=(me_r, peer),
                    device_id_type=MESH,
                )
            )
            copies[-1].start()
        return copies

    def from_peers(source, target, send_sem, recv_sem):
        for k, peer in enumerate(peers):
            pltpu.make_async_remote_copy(
                src_ref=source(peer),
                dst_ref=target(peer),
                send_sem=send_sem.at[k],
                recv_sem=recv_sem.at[peer],
                device_id=(me_r, peer),
                device_id_type=MESH,
            ).wait_recv()

    kinds = ((downs, down_send, down_recv, []), (ups, up_send, up_recv, []))
    down, up = kinds

    def map_copy(kind, slot, device, index):
        blocks, send_sem, recv_sem, _ = kind
        return pltpu.make_async_remote_copy(
            src_ref=blocks.at[slot],
            dst_ref=blocks.at[slot],
            send_sem=send_sem.at[index],
            recv_sem=recv_sem.at[slot],
            device_id=(device, me_t),
            device_id_type=MESH,
        )

    def send_map(kind, slot, device):
        copy = map_copy(kind, slot, device, len(kind[3]))
        kind[3].append(copy)
        copy.start()

    def wait_map(kind, slot):
        map_copy(kind, slot, at(0, 1), 0).wait_recv()

    token_args = (
        lambda peer: tokens.at[own_rows],
        lambda t: tokens.at[pl.ds(pl.multiple_of(t * pad, pad), pad)],
        tok_send,
        tok_recv,
    )
    half = NZ // 2
    x_next, x_last = at(1, 0), at(-1, 0)
    stages = -(-half // STRIDE)
    arrived = set()

    def wait_once(kind, dz):
        if dz != 0 and (id(kind), dz) not in arrived:
            arrived.add((id(kind), dz))
            wait_map(kind, at(0, dz))

    def z_send(kind, stage):
        base = stage * STRIDE
        for sign, reach in ((1, half), (-1, half - 1)):
            steps = range(min(base + STRIDE, reach), base, -1)
            if len(steps):
                wait_once(kind, -sign * base)
            for to in steps:
                send_map(kind, at(0, -sign * base), at(0, sign * (to - base)))

    def members(stage):
        if stage == 0:
            return [0]
        near = range((stage - 1) * STRIDE + 1, min(stage * STRIDE, half) + 1)
        return [dz for d in near for dz in ((-d, d) if d < half else (-d,))]

    def x_send(kind, stage):
        for dz in members(stage):
            wait_once(kind, dz)
            if kind is down:
                send_map(kind, at(0, dz), at(2, 0))
            send_map(kind, at(0, dz), x_next)
            send_map(kind, at(0, dz), x_last)

    def x_pass(kind, stage):
        for dz in members(stage):
            wait_map(kind, at(-1, dz))
            if kind is up and dz <= 0:
                send_map(kind, at(-1, dz), x_next)
            wait_map(kind, at(1, dz))
            if kind is up and dz > 0:
                send_map(kind, at(1, dz), x_last)

    def x_finish(kind):
        for stage in range(stages + 1):
            for dz in members(stage):
                wait_map(kind, at(2, dz))

    for kind in kinds:
        z_send(kind, 0)
    token_copies = to_peers(*token_args)
    for kind in kinds:
        x_send(kind, 0)
    for stage in range(1, stages + 1):
        for kind in kinds:
            z_send(kind, stage)
        for kind in kinds:
            x_send(kind, stage)
        if stage == stages:
            break
        for kind in kinds:
            x_pass(kind, stage - 1)
        if stage == stages - 1:
            from_peers(*token_args)
            loads[0].wait()
            v = jnp.dot(tokens[...], gate_w[...], preferred_element_type=jnp.float32)
            v = v * gate_scale_ref[...][None]
            gate_pre[...] = v / (1.0 + jnp.exp(-v))
            loads[1].wait()
            up_base[...] = jnp.dot(tokens[...], up_w[...], preferred_element_type=jnp.float32)
    for stage in (stages - 1, stages):
        x_pass(down, stage)
    x_pass(up, stages - 1)
    x_finish(down)

    lane = lax.broadcasted_iota(jnp.int32, (token_count, window), 1)
    token_share = tokens[:, pl.ds(start, window)].astype(jnp.float32)
    token_share = jnp.where((lane >= offset) & (lane < offset + share), token_share, 0.0)
    token_share = token_share.astype(jnp.bfloat16)
    products = lax.dot_general(
        downs[...].reshape(owners * rank, window),
        token_share,
        (((1,), (1,)), ((), ())),
        preferred_element_type=jnp.float32,
    ).reshape(owners, rank, token_count)
    partial = jnp.sum(jnp.where(chosen, products, 0.0), axis=0)
    sums_out[...] = partial
    sum_args = (lambda peer: sums_out, lambda t: sums_in.at[t], sum_send, sum_recv)
    sum_copies = to_peers(*sum_args)
    x_pass(up, stages)
    x_finish(up)
    from_peers(*sum_args)
    shrink = partial
    for peer in peers:
        shrink = shrink + sums_in[peer]
    shrink = shrink.astype(jnp.bfloat16).astype(jnp.float32)
    spread = jnp.where(chosen, shrink[None], 0.0).astype(jnp.bfloat16)
    delta = lax.dot_general(
        spread.reshape(owners * rank, token_count),
        ups[...].reshape(owners * rank, columns),
        (((0,), (0,)), ((), ())),
        preferred_element_type=jnp.float32,
    )
    delta = delta.astype(jnp.bfloat16).astype(jnp.float32)
    up_pre = (up_base[...] + 0.5 * delta) * up_scale_ref[...][None]
    inner = (gate_pre[...] * up_pre).astype(jnp.bfloat16)
    loads[2].wait()
    gate_rows = jnp.dot(inner, down_w[...], preferred_element_type=jnp.float32)
    part_out[...] = gate_rows.astype(jnp.bfloat16).reshape(tp_count, pad, features)
    part_args = (lambda peer: part_out.at[peer], lambda t: part_in.at[t], part_send, part_recv)
    part_copies = to_peers(*part_args)

    begin = rms_norm(tokens[own_rows, :].astype(jnp.float32))
    branch = part_out[me_t].astype(jnp.float32)
    from_peers(*part_args)
    for peer in peers:
        branch = branch + part_in[peer].astype(jnp.float32)
    mixed = begin + step_ref[...][None] * (rms_norm(branch) - begin)
    row = lax.broadcasted_iota(jnp.int32, (pad, features), 0)
    out_ref[...] = jnp.where(row < lengths_ref[me_t], rms_norm(mixed), 0.0).astype(jnp.bfloat16)
    for copy in token_copies + sum_copies + part_copies + down[3] + up[3]:
        copy.wait_send()


def body(
    hidden,
    gate_weight,
    up_weight,
    down_weight,
    gate_scale,
    up_scale,
    update_step_size,
    adapter_down_maps,
    adapter_up_maps,
    lengths,
    request_adapter_index,
):
    tp_count = lax.axis_size("tp")
    owners = lax.axis_size("req")
    pad, features = hidden.shape
    rank, columns = adapter_up_maps.shape[1:]
    token_count = tp_count * pad
    bf16, f32 = jnp.bfloat16, jnp.float32
    vmem = pl.BlockSpec(memory_space=pltpu.VMEM)
    hbm = pl.BlockSpec(memory_space=pl.ANY)
    dma = pltpu.SemaphoreType.DMA
    return pl.pallas_call(
        functools.partial(kernel, tp_count),
        out_shape=jax.ShapeDtypeStruct((pad, features), bf16),
        in_specs=[hbm] * 11,
        out_specs=vmem,
        scratch_shapes=[
            pltpu.VMEM((token_count, features), bf16),
            pltpu.VMEM(gate_weight.shape, bf16),
            pltpu.VMEM(up_weight.shape, bf16),
            pltpu.VMEM(down_weight.shape, bf16),
            pltpu.VMEM(gate_scale.shape, f32),
            pltpu.VMEM(up_scale.shape, f32),
            pltpu.VMEM(update_step_size.shape, f32),
            pltpu.SMEM(lengths.shape, jnp.int32),
            pltpu.SMEM(lengths.shape, jnp.int32),
            pltpu.VMEM((token_count, columns), f32),
            pltpu.VMEM((token_count, columns), f32),
            pltpu.VMEM((owners, rank, 256), bf16),
            pltpu.VMEM((owners, rank, columns), bf16),
            pltpu.VMEM((rank, token_count), f32),
            pltpu.VMEM((tp_count, rank, token_count), f32),
            pltpu.VMEM((tp_count, pad, features), bf16),
            pltpu.VMEM((tp_count, pad, features), bf16),
            dma((11,)),
            dma((tp_count - 1,)),
            dma((tp_count,)),
            dma((owners - 1,)),
            dma((owners,)),
            dma((owners - 1,)),
            dma((owners,)),
            dma((tp_count - 1,)),
            dma((tp_count,)),
            dma((tp_count - 1,)),
            dma((tp_count,)),
        ],
        compiler_params=pltpu.CompilerParams(
            collective_id=0, has_side_effects=True, vmem_limit_bytes=67000000
        ),
    )(
        hidden,
        gate_weight,
        up_weight,
        down_weight,
        gate_scale,
        up_scale,
        update_step_size,
        adapter_down_maps.transpose(0, 2, 1)[0],
        adapter_up_maps[0],
        lengths,
        request_adapter_index,
    )


def solution(mesh):
    placed = (
        P(("req", "tp"), None),
        P(None, "tp"),
        P(None, "tp"),
        P("tp", None),
        P("tp"),
        P("tp"),
        P(),
        P("req", None, None),
        P("req", None, "tp"),
        P("req"),
        P("req"),
    )
    return jax.shard_map(
        body, mesh=mesh, in_specs=placed, out_specs=P(("req", "tp"), None), check_vma=False
    )
```

```python
import functools

import jax
import jax.numpy as jnp
from jax import lax
from jax.experimental import pallas as pl
from jax.experimental.pallas import tpu as pltpu
from jax.sharding import PartitionSpec as P

MESH = pl.DeviceIdType.MESH
NX, NZ = 4, 16
STRIDE = 2
EPS = 1e-06


def rms_norm(values):
    return values * lax.rsqrt(jnp.mean(values * values, axis=-1, keepdims=True) + EPS)


def kernel(
    tp_count,
    hidden_hbm,
    gate_hbm,
    up_hbm,
    down_hbm,
    gate_scale_hbm,
    up_scale_hbm,
    step_hbm,
    down_map_hbm,
    up_map_hbm,
    lengths_hbm,
    ids_hbm,
    out_ref,
    tokens,
    gate_w,
    up_w,
    down_w,
    gate_scale_ref,
    up_scale_ref,
    step_ref,
    lengths_ref,
    ids_ref,
    gate_pre,
    up_base,
    downs,
    ups,
    sums_out,
    sums_in,
    part_out,
    part_in,
    load_sem,
    tok_send,
    tok_recv,
    down_send,
    down_recv,
    up_send,
    up_recv,
    sum_send,
    sum_recv,
    part_send,
    part_recv,
):
    me_r = lax.axis_index("req")
    me_t = lax.axis_index("tp")
    x = me_r // NZ
    z = lax.rem(me_r, NZ)
    pad, features = hidden_hbm.shape
    rank, columns = up_map_hbm.shape
    owners, _, window = downs.shape
    token_count = tp_count * pad
    y, core = me_t // 2, lax.rem(me_t, 2)
    hops = [(dy, other) for dy in (2, 1, 3) for other in (0, 1)] + [(0, 1)]
    peers = [lax.rem(y + dy, tp_count // 2) * 2 + lax.rem(core + other, 2) for dy, other in hops]

    def at(dx, dz):
        return lax.rem(x + dx + NX, NX) * NZ + lax.rem(z + dz + NZ, NZ)

    barrier = pltpu.get_barrier_semaphore()
    for peer in peers:
        pl.semaphore_signal(barrier, inc=1, device_id=(me_r, peer), device_id_type=MESH)
    near = [(0, sign * d) for d in range(1, STRIDE + 1) for sign in (1, -1)] + [(1, 0), (-1, 0), (2, 0)]
    for dx, dz in near:
        pl.semaphore_signal(barrier, inc=1, device_id=(at(dx, dz), me_t), device_id_type=MESH)

    share = features // tp_count
    start = pl.multiple_of((me_t * share) // 128 * 128, 128)
    offset = me_t * share - start
    own_rows = pl.ds(pl.multiple_of(me_t * pad, pad), pad)
    loads = [
        pltpu.make_async_copy(source, target, load_sem.at[i])
        for i, (source, target) in enumerate(
            (
                (gate_hbm, gate_w),
                (up_hbm, up_w),
                (down_hbm, down_w),
                (hidden_hbm, tokens.at[own_rows]),
                (up_map_hbm, ups.at[me_r]),
                (down_map_hbm.at[:, pl.ds(start, window)], downs.at[me_r]),
                (lengths_hbm, lengths_ref),
                (ids_hbm, ids_ref),
                (gate_scale_hbm, gate_scale_ref),
                (up_scale_hbm, up_scale_ref),
                (step_hbm, step_ref),
            )
        )
    ]
    for i in (3, 4, 5, 6, 7, 8, 9, 10, 0, 1, 2):
        loads[i].start()
    for i in (6, 7, 8, 9, 10):
        loads[i].wait()

    lane = lax.broadcasted_iota(jnp.int32, (1, token_count), 1)
    token_ids = jnp.full((1, token_count), -1, jnp.int32)
    for s in range(tp_count):
        inside = (lane >= s * pad) & (lane < s * pad + lengths_ref[s])
        token_ids = jnp.where(inside, ids_ref[s], token_ids)
    owner_ids = lax.broadcasted_iota(jnp.int32, (owners, 1, token_count), 0)
    chosen = owner_ids == token_ids[None]

    for i in (3, 4, 5):
        loads[i].wait()
    pl.semaphore_wait(barrier, tp_count - 1 + len(near))

    def to_peers(source, target, send_sem, recv_sem):
        copies = []
        for k, peer in enumerate(peers):
            copies.append(
                pltpu.make_async_remote_copy(
                    src_ref=source(peer),
                    dst_ref=target(me_t),
                    send_sem=send_sem.at[k],
                    recv_sem=recv_sem.at[me_t],
                    device_id=(me_r, peer),
                    device_id_type=MESH,
                )
            )
            copies[-1].start()
        return copies

    def from_peers(source, target, send_sem, recv_sem):
        for k, peer in enumerate(peers):
            pltpu.make_async_remote_copy(
                src_ref=source(peer),
                dst_ref=target(peer),
                send_sem=send_sem.at[k],
                recv_sem=recv_sem.at[peer],
                device_id=(me_r, peer),
                device_id_type=MESH,
            ).wait_recv()

    kinds = ((downs, down_send, down_recv, []), (ups, up_send, up_recv, []))
    down, up = kinds

    def map_copy(kind, slot, device, index):
        blocks, send_sem, recv_sem, _ = kind
        return pltpu.make_async_remote_copy(
            src_ref=blocks.at[slot],
            dst_ref=blocks.at[slot],
            send_sem=send_sem.at[index],
            recv_sem=recv_sem.at[slot],
            device_id=(device, me_t),
            device_id_type=MESH,
        )

    def send_map(kind, slot, device):
        copy = map_copy(kind, slot, device, len(kind[3]))
        kind[3].append(copy)
        copy.start()

    def wait_map(kind, slot):
        map_copy(kind, slot, at(0, 1), 0).wait_recv()

    token_args = (
        lambda peer: tokens.at[own_rows],
        lambda t: tokens.at[pl.ds(pl.multiple_of(t * pad, pad), pad)],
        tok_send,
        tok_recv,
    )
    half = NZ // 2
    x_next, x_last = at(1, 0), at(-1, 0)
    stages = -(-half // STRIDE)
    arrived = set()

    def wait_once(kind, dz):
        if dz != 0 and (id(kind), dz) not in arrived:
            arrived.add((id(kind), dz))
            wait_map(kind, at(0, dz))

    def z_send(kind, stage):
        base = stage * STRIDE
        for sign, reach in ((1, half), (-1, half - 1)):
            steps = range(min(base + STRIDE, reach), base, -1)
            if len(steps):
                wait_once(kind, -sign * base)
            for to in steps:
                send_map(kind, at(0, -sign * base), at(0, sign * (to - base)))

    def members(stage):
        if stage == 0:
            return [0]
        near = range((stage - 1) * STRIDE + 1, min(stage * STRIDE, half) + 1)
        return [dz for d in near for dz in ((-d, d) if d < half else (-d,))]

    def x_send(kind, stage):
        for dz in members(stage):
            wait_once(kind, dz)
            if kind is down:
                send_map(kind, at(0, dz), at(2, 0))
            send_map(kind, at(0, dz), x_next)
            send_map(kind, at(0, dz), x_last)

    def x_pass(kind, stage):
        for dz in members(stage):
            wait_map(kind, at(-1, dz))
            if kind is up and dz <= 0:
                send_map(kind, at(-1, dz), x_next)
            wait_map(kind, at(1, dz))
            if kind is up and dz > 0:
                send_map(kind, at(1, dz), x_last)

    def x_finish(kind):
        for stage in range(stages + 1):
            for dz in members(stage):
                wait_map(kind, at(2, dz))

    for kind in kinds:
        z_send(kind, 0)
    token_copies = to_peers(*token_args)
    for kind in kinds:
        x_send(kind, 0)
    for stage in range(1, stages + 1):
        for kind in kinds:
            z_send(kind, stage)
        for kind in kinds:
            x_send(kind, stage)
        if stage == stages:
            break
        for kind in kinds:
            x_pass(kind, stage - 1)
        if stage == stages - 1:
            from_peers(*token_args)
            loads[0].wait()
            v = jnp.dot(tokens[...], gate_w[...], preferred_element_type=jnp.float32)
            v = v * gate_scale_ref[...][None]
            gate_pre[...] = v / (1.0 + jnp.exp(-v))
    for stage in (stages - 1, stages):
        x_pass(down, stage)
    x_pass(up, stages - 1)
    x_finish(down)

    lane = lax.broadcasted_iota(jnp.int32, (token_count, window), 1)
    token_share = tokens[:, pl.ds(start, window)].astype(jnp.float32)
    token_share = jnp.where((lane >= offset) & (lane < offset + share), token_share, 0.0)
    token_share = token_share.astype(jnp.bfloat16)
    products = lax.dot_general(
        downs[...].reshape(owners * rank, window),
        token_share,
        (((1,), (1,)), ((), ())),
        preferred_element_type=jnp.float32,
    ).reshape(owners, rank, token_count)
    partial = jnp.sum(jnp.where(chosen, products, 0.0), axis=0)
    sums_out[...] = partial
    sum_args = (lambda peer: sums_out, lambda t: sums_in.at[t], sum_send, sum_recv)
    sum_copies = to_peers(*sum_args)
    x_pass(up, stages)
    loads[1].wait()
    up_base[...] = jnp.dot(tokens[...], up_w[...], preferred_element_type=jnp.float32)
    x_finish(up)
    from_peers(*sum_args)
    shrink = partial
    for peer in peers:
        shrink = shrink + sums_in[peer]
    shrink = shrink.astype(jnp.bfloat16).astype(jnp.float32)
    spread = jnp.where(chosen, shrink[None], 0.0).astype(jnp.bfloat16)
    delta = lax.dot_general(
        spread.reshape(owners * rank, token_count),
        ups[...].reshape(owners * rank, columns),
        (((0,), (0,)), ((), ())),
        preferred_element_type=jnp.float32,
    )
    delta = delta.astype(jnp.bfloat16).astype(jnp.float32)
    up_pre = (up_base[...] + 0.5 * delta) * up_scale_ref[...][None]
    inner = (gate_pre[...] * up_pre).astype(jnp.bfloat16)
    loads[2].wait()
    gate_rows = jnp.dot(inner, down_w[...], preferred_element_type=jnp.float32)
    part_out[...] = gate_rows.astype(jnp.bfloat16).reshape(tp_count, pad, features)
    part_args = (lambda peer: part_out.at[peer], lambda t: part_in.at[t], part_send, part_recv)
    part_copies = to_peers(*part_args)

    begin = rms_norm(tokens[own_rows, :].astype(jnp.float32))
    branch = part_out[me_t].astype(jnp.float32)
    from_peers(*part_args)
    for peer in peers:
        branch = branch + part_in[peer].astype(jnp.float32)
    mixed = begin + step_ref[...][None] * (rms_norm(branch) - begin)
    row = lax.broadcasted_iota(jnp.int32, (pad, features), 0)
    out_ref[...] = jnp.where(row < lengths_ref[me_t], rms_norm(mixed), 0.0).astype(jnp.bfloat16)
    for copy in token_copies + sum_copies + part_copies + down[3] + up[3]:
        copy.wait_send()


def body(
    hidden,
    gate_weight,
    up_weight,
    down_weight,
    gate_scale,
    up_scale,
    update_step_size,
    adapter_down_maps,
    adapter_up_maps,
    lengths,
    request_adapter_index,
):
    tp_count = lax.axis_size("tp")
    owners = lax.axis_size("req")
    pad, features = hidden.shape
    rank, columns = adapter_up_maps.shape[1:]
    token_count = tp_count * pad
    bf16, f32 = jnp.bfloat16, jnp.float32
    vmem = pl.BlockSpec(memory_space=pltpu.VMEM)
    hbm = pl.BlockSpec(memory_space=pl.ANY)
    dma = pltpu.SemaphoreType.DMA
    return pl.pallas_call(
        functools.partial(kernel, tp_count),
        out_shape=jax.ShapeDtypeStruct((pad, features), bf16),
        in_specs=[hbm] * 11,
        out_specs=vmem,
        scratch_shapes=[
            pltpu.VMEM((token_count, features), bf16),
            pltpu.VMEM(gate_weight.shape, bf16),
            pltpu.VMEM(up_weight.shape, bf16),
            pltpu.VMEM(down_weight.shape, bf16),
            pltpu.VMEM(gate_scale.shape, f32),
            pltpu.VMEM(up_scale.shape, f32),
            pltpu.VMEM(update_step_size.shape, f32),
            pltpu.SMEM(lengths.shape, jnp.int32),
            pltpu.SMEM(lengths.shape, jnp.int32),
            pltpu.VMEM((token_count, columns), f32),
            pltpu.VMEM((token_count, columns), f32),
            pltpu.VMEM((owners, rank, 256), bf16),
            pltpu.VMEM((owners, rank, columns), bf16),
            pltpu.VMEM((rank, token_count), f32),
            pltpu.VMEM((tp_count, rank, token_count), f32),
            pltpu.VMEM((tp_count, pad, features), bf16),
            pltpu.VMEM((tp_count, pad, features), bf16),
            dma((11,)),
            dma((tp_count - 1,)),
            dma((tp_count,)),
            dma((owners - 1,)),
            dma((owners,)),
            dma((owners - 1,)),
            dma((owners,)),
            dma((tp_count - 1,)),
            dma((tp_count,)),
            dma((tp_count - 1,)),
            dma((tp_count,)),
        ],
        compiler_params=pltpu.CompilerParams(
            collective_id=0, has_side_effects=True, vmem_limit_bytes=67000000
        ),
    )(
        hidden,
        gate_weight,
        up_weight,
        down_weight,
        gate_scale,
        up_scale,
        update_step_size,
        adapter_down_maps.transpose(0, 2, 1)[0],
        adapter_up_maps[0],
        lengths,
        request_adapter_index,
    )


def solution(mesh):
    placed = (
        P(("req", "tp"), None),
        P(None, "tp"),
        P(None, "tp"),
        P("tp", None),
        P("tp"),
        P("tp"),
        P(),
        P("req", None, None),
        P("req", None, "tp"),
        P("req"),
        P("req"),
    )
    return jax.shard_map(
        body, mesh=mesh, in_specs=placed, out_specs=P(("req", "tp"), None), check_vma=False
    )
```
